32 devices in a mesh: grp: 2 (over y), feat: 4 (over z), samp: 4 (over x, core).
Axes of the slice: x: 2, y: 2, z: 4, core: 2. Of those that a mesh axis runs over, the one named last changes fastest.
Arguments:
- embeddings: bfloat16 [8192, 1024], P(('grp', 'samp')), parts along dimension 0, may hold values from -6 to 6
- sign_bits: int32 [4096], P('feat'), may hold values 0 or 1
- perms: int32 [4, 1024], P('feat'), may hold values from 0 to 1023, each once within a row
- gauss: float32 [4096], P('feat'), may hold values from -4 to 4
- scale: float32 [4096], P('feat'), may hold values from 0.5 to 2
- phase: float32 [4096], P('feat'), may hold values from -3.140625 to 3.140625
- basis: float32 [128, 4096], P('grp', 'feat'), parts along dimension 0, may hold values from -40 to 40
Outputs:
- basis_out: float32 [128, 4096], P('grp', 'feat'), parts along dimension 0
- projections: float32 [128, 4096], P('grp', 'samp'), parts along dimension 0
The draws below stay inside these ranges and needn't reach their ends.
There are 2 independent parts, one for each index of `grp`. The reference program is written for one: setup_inputs(seed, part) draws one part's arguments, and reference() takes and returns one part's arrays. A program takes and returns all parts, laid end to end along the dimension named above; an argument that names none is the same for every part. Nothing has to cross between parts.
Inputs may be any that keep to these rules, and one draw needn't show every extreme that they name: Each row of perms names every number of 0 to 1023 once.
All inputs are finite; a program needn't handle non-finite values. No bound on the sum of `sign_bits` on one device may be relied on, other than what follows from the above.
Results may differ from the reference program's by a relative error of at most 0.0057.
Values sent between devices are 32-bit elements; how exact they have to be, the bound alone decides.
A program may use at most 64 MiB of HBM per device.

```python
import math
import jax
import jax.numpy as jnp
from jax import lax

D = 1024
K = 64
BLOCKS = 4
FEATURES = 4096
SPAN = 4096


def draw_basis(key, part):
    base = jax.random.normal(jax.random.fold_in(key, 11), (K, FEATURES), jnp.float32)
    where = jnp.arange(FEATURES, dtype=jnp.float32)[None, :] / (FEATURES - 1)
    rising = jnp.exp(math.log(6.0) * where)
    return jnp.clip(base, -6.0, 6.0) * rising


def touch_ends(drawn, key, low, top_value):
    longest = drawn.shape.index(max(drawn.shape))
    spots = []
    for shift in (0, 1):
        where = [jax.random.randint(jax.random.fold_in(key, axis), (), 0, length) for axis, length in enumerate(drawn.shape)]
        where[longest] = (where[longest] + shift) % drawn.shape[longest]
        spots.append(tuple(where))
    return drawn.at[spots[0]].set(low).at[spots[1]].set(top_value)


def shard_levels(own_key, dims, shards, smallest, largest):
    def one(axis_at, shards_of):
        steps = jax.random.uniform(jax.random.fold_in(jax.random.fold_in(own_key, 6), axis_at), (shards_of,), jnp.float32, smallest / len(shards), largest / len(shards))
        return jnp.repeat(jnp.exp(steps), dims[axis_at] // shards_of).reshape((-1,) + (1,) * (len(dims) - axis_at - 1))

    loudness = one(*shards[0])
    for cut in shards[1:]:
        loudness = loudness * one(*cut)
    return loudness


def scatter_about(rng, dims, scale, limit, split=(), kind=jnp.bfloat16):
    values = jax.random.normal(rng, dims, jnp.float32) * scale
    if len(split) > 0:
        values = shard_levels(rng, dims, split, -0.22, 0.18) * values
    return jnp.clip(values, min=-limit, max=limit).astype(kind)


def setup_inputs(seed: int = 0, part: int = 0) -> dict:
    key_list = jax.random.split(jax.random.key(seed), 8)
    own_keys = jax.random.split(jax.random.fold_in(key_list[7], part), 8)
    return {
        "embeddings": scatter_about(own_keys[0], (SPAN, D), 1.0, 6.0, ((0, 4),)),
        "sign_bits": touch_ends((jax.random.randint(key_list[1], (FEATURES,), 0, 2) < 1).astype(jnp.int32), jax.random.fold_in(key_list[1], 1), 0, 1),
        "perms": jax.vmap(lambda own: jax.random.permutation(own, D))(jax.random.split(key_list[2], BLOCKS)).reshape((BLOCKS, D)).astype(jnp.int32),
        "gauss": scatter_about(key_list[3], (FEATURES,), 1.0, 4.0, ((0, 4),), jnp.float32),
        "scale": jnp.clip(jnp.exp(math.log(2.0) - 1.3862944 * jax.random.uniform(key_list[4], (FEATURES,), jnp.float32) ** shard_levels(key_list[4], (FEATURES,), ((0, 4),), -0.2, 0.2)), 0.5, 2.0),
        "phase": jnp.clip(jax.random.uniform(key_list[5], (FEATURES,), jnp.float32, -3.140625, 3.140625), -3.140625, 3.140625),
        "basis": draw_basis(jax.random.fold_in(jax.random.fold_in(key_list[7], part), 71), part),
    }


def walsh(values):
    width = values.shape[-1]
    leading = values.shape[:-1]
    stride = 1
    while stride < width:
        folded = values.reshape(leading + (width // (2 * stride), 2, stride))
        upper = folded[..., 0, :]
        lower = folded[..., 1, :]
        values = jnp.stack([upper + lower, upper - lower], axis=-2).reshape(leading + (width,))
        stride = stride * 2
    return values

def block_features(embeddings, bits, order, gauss, scale, phase):
    signs = (2 * bits - 1).astype(jnp.bfloat16)
    first = walsh((embeddings * signs).astype(jnp.float32)).astype(jnp.bfloat16)
    picked = jnp.take(first, order, axis=1)
    mixed = (picked.astype(jnp.float32) * gauss).astype(jnp.bfloat16)
    freq = walsh(mixed.astype(jnp.float32)) * scale / D + phase
    return (math.sqrt(2.0) * jnp.cos(freq)).astype(jnp.bfloat16)

def features_of(block, embeddings, sign_bits, perms, gauss, scale, phase):
    start = (block * D).astype(jnp.int32)
    return block_features(embeddings, lax.dynamic_slice_in_dim(sign_bits, start, D), perms[block], lax.dynamic_slice_in_dim(gauss, start, D), lax.dynamic_slice_in_dim(scale, start, D), lax.dynamic_slice_in_dim(phase, start, D))

def orthonormal(grown):
    gram = jnp.dot(grown, grown.T, precision=lax.Precision.HIGHEST) / FEATURES
    lower = jnp.linalg.cholesky(gram)
    return jax.scipy.linalg.solve_triangular(lower, grown, lower=True)

def reference(embeddings, sign_bits, perms, gauss, scale, phase, basis):
    basis_low = basis.astype(jnp.bfloat16)
    blocks = jnp.arange(BLOCKS, dtype=jnp.int32)

    def score_step(total, block):
        feats = features_of(block, embeddings, sign_bits, perms, gauss, scale, phase)
        piece = lax.dynamic_slice_in_dim(basis_low, (block * D).astype(jnp.int32), D, 1)
        return (total + jnp.dot(piece.astype(jnp.float32), feats.T.astype(jnp.float32), preferred_element_type=jnp.float32), None)
    total, _ = lax.scan(score_step, jnp.zeros((K, SPAN), jnp.float32), blocks)
    projections = total / math.sqrt(FEATURES)
    proj_low = projections.astype(jnp.bfloat16)

    def update_block(block):
        feats = features_of(block, embeddings, sign_bits, perms, gauss, scale, phase)
        return jnp.dot(proj_low.astype(jnp.float32), feats.astype(jnp.float32), preferred_element_type=jnp.float32)
    update = lax.map(update_block, blocks)
    update = jnp.transpose(update, (1, 0, 2)).reshape(K, FEATURES)
    grown = basis + update / math.sqrt(SPAN)
    basis_out = orthonormal(grown)
    return (basis_out, projections)
```

```python
import functools
import math

import jax
import jax.numpy as jnp
import numpy as np
from jax import lax
from jax.experimental import pallas as pl
from jax.experimental.pallas import tpu as pltpu
from jax.sharding import PartitionSpec as P

MESH = pl.DeviceIdType.MESH
BLOCK = 256
HIGHEST = lax.Precision.HIGHEST


def cosine_coefficients(degree):
    nodes = np.cos(np.pi * (np.arange(400) + 0.5) / 400)
    squares = (nodes + 1) / 8
    fitted = np.polynomial.Chebyshev.fit(
        squares, np.cos(2 * np.pi * np.sqrt(squares)), degree, domain=[0, 0.25]
    )
    return [float(c) * math.sqrt(2.0) for c in fitted.convert(kind=np.polynomial.Polynomial).coef]


COS = cosine_coefficients(6)


def parity_sign(bits):
    for shift in (8, 4, 2, 1):
        bits = bits ^ jnp.right_shift(bits, shift)
    return (1 - 2 * (bits & 1)).astype(jnp.float32)


def scaled_cosine(turns):
    rest = turns - jnp.round(turns)
    square = rest * rest
    total = jnp.full_like(square, COS[-1])
    for c in COS[-2::-1]:
        total = total * square + c
    return total


def transform(blocks):
    stride = 1
    while stride < len(blocks):
        result = list(blocks)
        for i in range(len(blocks)):
            if not i & stride:
                result[i] = blocks[i] + blocks[i + stride]
                result[i + stride] = blocks[i] - blocks[i + stride]
        blocks = result
        stride *= 2
    return blocks


def inverse_factor(gram):
    size = gram.shape[0]
    row = lax.broadcasted_iota(jnp.int32, (8, size), 0)
    lane = lax.broadcasted_iota(jnp.int32, (8, size), 1)
    width = 2 * size
    sub = lax.broadcasted_iota(jnp.int32, (8, width), 0)
    groups = [
        jnp.concatenate(
            [(lane == row + 8 * g).astype(jnp.float32), gram[8 * g : 8 * g + 8]], axis=1
        )
        for g in range(size // 8)
    ]
    pivots = [jnp.ones((8, width), jnp.float32) for _ in groups]
    step = 4
    for first in range(0, size, step):
        own = first // 8
        at = first % 8
        live = range(own, size // 8)
        rows = [
            jnp.broadcast_to(groups[own][at + k : at + k + 1], (8, width)) for k in range(step)
        ]
        cols = [
            {
                g: jnp.broadcast_to(
                    groups[g][:, size + first + k : size + first + k + 1], (8, width)
                )
                for g in live
            }
            for k in range(step)
        ]
        cross = [
            [
                jnp.broadcast_to(cols[m][own][at + k : at + k + 1], (8, width))
                for m in range(step)
            ]
            for k in range(step)
        ]
        for k in range(step):
            inverse = 1.0 / cross[k][k]
            pivots[own] = jnp.where(sub == at + k, cross[k][k], pivots[own])
            for later in range(k + 1, step):
                factor = cross[later][k] * inverse
                rows[later] = rows[later] - factor * rows[k]
                share = cross[k][later] * inverse
                for g in live:
                    cols[later][g] = cols[later][g] - share * cols[k][g]
                for m in range(k + 1, step):
                    cross[later][m] = cross[later][m] - factor * cross[k][m]
            for g in live:
                weight = cols[k][g] * inverse
                if g == own:
                    weight = jnp.where(sub > at + k, weight, 0.0)
                groups[g] = groups[g] - weight * rows[k]
    scaled = [g / jnp.sqrt(p) for g, p in zip(groups, pivots)]
    return jnp.concatenate(scaled, axis=0)[:, :size]


def kernel(
    feats, samps, emb, bits, perm, gauss, scale, phase, basis, out, scores_out,
    table, small, features, score_send, score_recv, proj, upd_send, upd_recv, grown,
    gram_send, gram_recv,
    s1, r1, s2, r2, s3, r3, s4, r4, s5, r5,
):
    me = lax.axis_index("feat")
    my = lax.axis_index("samp")
    rows, width = emb.shape
    order = basis.shape[0]
    chunk = rows // feats
    span = width // samps
    barrier = pltpu.get_barrier_semaphore()
    for d in range(1, feats):
        pl.semaphore_signal(
            barrier, inc=1, device_id={"feat": lax.rem(me + d, feats)}, device_id_type=MESH
        )
    for d in range(1, samps):
        pl.semaphore_signal(
            barrier, inc=1, device_id={"samp": lax.rem(my + d, samps)}, device_id_type=MESH
        )

    places = perm[...]
    base = parity_sign(lax.broadcasted_iota(jnp.int32, (128, width), 0) & places & 127).astype(
        jnp.bfloat16
    )
    for a in range(width // 128):
        flips = parity_sign(jnp.right_shift(places, 7) & a).astype(jnp.bfloat16)
        table[a * 128 : (a + 1) * 128, :] = base * flips
    square = (BLOCK, BLOCK)
    small[...] = parity_sign(
        lax.broadcasted_iota(jnp.int32, square, 0) & lax.broadcasted_iota(jnp.int32, square, 1)
    ).astype(jnp.bfloat16)
    signs = (2 * bits[...] - 1).astype(jnp.float32).astype(jnp.bfloat16)
    gains = gauss[...]
    rate = scale[...] * (1.0 / (2.0 * math.pi * width))
    offset = phase[...] * (1.0 / (2.0 * math.pi))
    basis_low = basis[...].astype(jnp.bfloat16)

    pl.semaphore_wait(barrier, feats + samps - 2)

    def copy(src, dst, send, recv, axis, to):
        return pltpu.make_async_remote_copy(
            src_ref=src, dst_ref=dst, send_sem=send, recv_sem=recv,
            device_id={axis: to}, device_id_type=MESH,
        )

    def score_copy(to):
        return copy(score_send.at[to], score_recv.at[me], s1.at[to], r1.at[me], "feat", to)

    def chunk_step(i, carry):
        at = lax.rem(me + 1 + i, feats)
        where = pl.ds(pl.multiple_of(at * chunk, chunk), chunk)
        signed = emb[where, :] * signs
        parts = []
        for n in range(width // BLOCK):
            cols = slice(n * BLOCK, (n + 1) * BLOCK)
            first = jnp.dot(signed, table[:, cols], preferred_element_type=jnp.float32)
            first = first.astype(jnp.bfloat16).astype(jnp.float32)
            mixed = (first * gains[:, cols]).astype(jnp.bfloat16)
            parts.append(jnp.dot(mixed, small[...], preferred_element_type=jnp.float32))
        for n, part in enumerate(transform(parts)):
            cols = slice(n * BLOCK, (n + 1) * BLOCK)
            turns = part * rate[:, cols] + offset[:, cols]
            features[where, cols] = scaled_cosine(turns).astype(jnp.bfloat16)
        score_send[at] = lax.dot_general(
            basis_low, features[where, :], (((1,), (1,)), ((), ())),
            preferred_element_type=jnp.float32,
        )

        @pl.when(i < feats - 1)
        def _():
            score_copy(at).start()

        return carry

    lax.fori_loop(0, feats, chunk_step, 0)

    total = score_send[me]
    for d in range(1, feats):
        source = lax.rem(me + d, feats)
        copy(
            score_send.at[source], score_recv.at[source], s1.at[source], r1.at[source],
            "feat", source,
        ).wait_recv()
        total = total + score_recv[source]
    proj[me] = total * (1.0 / math.sqrt(width * feats))

    def proj_copy(slot, to):
        return copy(proj.at[slot], proj.at[slot], s2.at[to], r2.at[slot], "feat", to)

    for d in range(1, feats):
        proj_copy(me, lax.rem(me + d, feats)).start()

    def add_rows(slot, first):
        where = pl.ds(pl.multiple_of(slot * chunk, chunk), chunk)
        low = proj[slot].astype(jnp.bfloat16)
        for q in range(samps):
            term = jnp.dot(
                low, features[where, q * span : (q + 1) * span],
                preferred_element_type=jnp.float32,
            )
            upd_send[q] = term if first else upd_send[q] + term

    add_rows(me, True)
    for d in range(1, feats):
        source = lax.rem(me + d, feats)
        proj_copy(source, source).wait_recv()
        add_rows(source, False)

    def upd_copy(to):
        return copy(upd_send.at[to], upd_recv.at[my], s3.at[to], r3.at[my], "samp", to)

    for d in range(1, samps):
        upd_copy(lax.rem(my + d, samps)).start()
    for slot in range(feats):
        scores_out[:, slot * chunk : (slot + 1) * chunk] = proj[slot]
    total = upd_send[my]
    for d in range(1, samps):
        source = lax.rem(my + d, samps)
        copy(
            upd_send.at[source], upd_recv.at[source], s3.at[source], r3.at[source],
            "samp", source,
        ).wait_recv()
        total = total + upd_recv[source]
    own_cols = pl.ds(pl.multiple_of(my * span, span), span)
    grown[my] = basis[:, own_cols] + total * (1.0 / math.sqrt(rows * samps))

    def grown_copy(slot, to):
        return copy(grown.at[slot], grown.at[slot], s4.at[to], r4.at[slot], "samp", to)

    for d in range(1, samps):
        grown_copy(my, lax.rem(my + d, samps)).start()

    def gram_of(slot):
        block = grown[slot]
        return lax.dot_general(
            block, block, (((1,), (1,)), ((), ())), precision=HIGHEST,
            preferred_element_type=jnp.float32,
        )

    gram = gram_of(my)
    for d in range(1, samps):
        source = lax.rem(my + d, samps)
        grown_copy(source, source).wait_recv()
        gram = gram + gram_of(source)

    half = order // 2
    packed = jnp.concatenate([gram[:half], gram[half:]], axis=1)
    gram_send[...] = packed

    def gram_copy(slot, to):
        return copy(gram_send, gram_recv.at[slot], s5.at[to], r5.at[slot], "feat", to)

    for d in range(1, feats):
        gram_copy(me, lax.rem(me + d, feats)).start()
    gram_recv[me] = packed
    for d in range(1, feats):
        source = lax.rem(me + d, feats)
        gram_copy(source, source).wait_recv()
    packed = gram_recv[0]
    for slot in range(1, feats):
        packed = packed + gram_recv[slot]
    packed = packed * (1.0 / (width * feats))
    gram = jnp.concatenate([packed[:, :order], packed[:, order:]], axis=0)
    inverse = inverse_factor(gram)
    for q in range(samps):
        out[:, q * span : (q + 1) * span] = jnp.dot(
            inverse, grown[q], precision=HIGHEST, preferred_element_type=jnp.float32
        )

    for d in range(1, feats):
        to = lax.rem(me + d, feats)
        score_copy(to).wait_send()
        proj_copy(me, to).wait_send()
        gram_copy(me, to).wait_send()
    for d in range(1, samps):
        to = lax.rem(my + d, samps)
        upd_copy(to).wait_send()
        grown_copy(my, to).wait_send()


def fused(feats, samps, embeddings, sign_bits, perms, gauss, scale, phase, basis):
    rows, width = embeddings.shape
    order = basis.shape[0]
    chunk, span = rows // feats, width // samps
    line = (1, width)
    whole = pl.BlockSpec(memory_space=pltpu.VMEM)
    f32, bf16, dma = jnp.float32, jnp.bfloat16, pltpu.SemaphoreType.DMA
    return pl.pallas_call(
        functools.partial(kernel, feats, samps),
        out_shape=(
            jax.ShapeDtypeStruct((order, width), f32),
            jax.ShapeDtypeStruct((order, rows), f32),
        ),
        in_specs=[whole] * 7,
        out_specs=(whole, whole),
        scratch_shapes=[
            pltpu.VMEM((width, width), bf16),
            pltpu.VMEM((BLOCK, BLOCK), bf16),
            pltpu.VMEM((rows, width), bf16),
            pltpu.VMEM((feats, order, chunk), f32),
            pltpu.VMEM((feats, order, chunk), f32),
            pltpu.VMEM((feats, order, chunk), f32),
            pltpu.VMEM((samps, order, span), f32),
            pltpu.VMEM((samps, order, span), f32),
            pltpu.VMEM((samps, order, span), f32),
            pltpu.VMEM((order // 2, 2 * order), f32),
            pltpu.VMEM((feats, order // 2, 2 * order), f32),
        ]
        + [dma((feats,))] * 4
        + [dma((samps,))] * 4
        + [dma((feats,))] * 2,
        compiler_params=pltpu.CompilerParams(
            collective_id=0, has_side_effects=True, vmem_limit_bytes=40 << 20
        ),
        name="oja",
    )(
        embeddings, sign_bits.reshape(line), perms.reshape(line), gauss.reshape(line),
        scale.reshape(line), phase.reshape(line), basis,
    )


def sylvester(width):
    indices = lax.iota(jnp.int32, width)
    return parity_sign(indices[:, None] & indices[None, :]).astype(jnp.bfloat16)


def general(embeddings, sign_bits, perms, gauss, scale, phase, basis):
    rows, width = embeddings.shape
    table = sylvester(width)
    features_total = width * lax.axis_size("feat")
    span_total = rows * lax.axis_size("samp")
    signs = (2 * sign_bits - 1).astype(jnp.bfloat16)
    columns = parity_sign(lax.iota(jnp.int32, width)[:, None] & perms[0][None, :]).astype(
        jnp.bfloat16
    )
    first = jnp.dot(embeddings * signs, columns, preferred_element_type=jnp.float32)
    mixed = (first.astype(jnp.bfloat16) * gauss).astype(jnp.bfloat16)
    freq = jnp.dot(mixed, table, preferred_element_type=jnp.float32) * scale / width + phase
    features = (math.sqrt(2.0) * jnp.cos(freq)).astype(jnp.bfloat16)
    partial_scores = lax.dot_general(
        basis.astype(jnp.bfloat16), features, (((1,), (1,)), ((), ())),
        preferred_element_type=jnp.float32,
    )
    projections = lax.psum(partial_scores, "feat") / math.sqrt(features_total)
    update_part = jnp.dot(
        projections.astype(jnp.bfloat16), features, preferred_element_type=jnp.float32
    )
    grown = basis + lax.psum(update_part, "samp") / math.sqrt(span_total)
    gram = lax.psum(jnp.dot(grown, grown.T, precision=HIGHEST), "feat")
    lower = jnp.linalg.cholesky(gram / features_total)
    return jax.scipy.linalg.solve_triangular(lower, grown, lower=True), projections


def solution(mesh):
    feats, samps = mesh.shape["feat"], mesh.shape["samp"]

    def local(embeddings, sign_bits, perms, gauss, scale, phase, basis):
        rows, width = embeddings.shape
        fits = (
            rows % (feats * 128) == 0
            and width % (samps * 128) == 0
            and width % BLOCK == 0
            and perms.shape[0] == 1
            and basis.shape[0] == 64
            and 1 < feats
            and 1 < samps
        )
        body = functools.partial(fused, feats, samps) if fits else general
        return body(embeddings, sign_bits, perms, gauss, scale, phase, basis)

    placed = (
        P(("grp", "samp"), None),
        P("feat"),
        P("feat", None),
        P("feat"),
        P("feat"),
        P("feat"),
        P("grp", "feat"),
    )
    return jax.shard_map(
        local,
        mesh=mesh,
        in_specs=placed,
        out_specs=(P("grp", "feat"), P("grp", "samp")),
        check_vma=False,
    )
```

```python
import functools
import math

import jax
import jax.numpy as jnp
import numpy as np
from jax import lax
from jax.experimental import pallas as pl
from jax.experimental.pallas import tpu as pltpu
from jax.sharding import PartitionSpec as P

MESH = pl.DeviceIdType.MESH
BLOCK = 256
HIGHEST = lax.Precision.HIGHEST


def cosine_coefficients(degree):
    nodes = np.cos(np.pi * (np.arange(400) + 0.5) / 400)
    squares = (nodes + 1) / 8
    fitted = np.polynomial.Chebyshev.fit(
        squares, np.cos(2 * np.pi * np.sqrt(squares)), degree, domain=[0, 0.25]
    )
    return [float(c) * math.sqrt(2.0) for c in fitted.convert(kind=np.polynomial.Polynomial).coef]


COS = cosine_coefficients(6)


def parity_sign(bits):
    for shift in (8, 4, 2, 1):
        bits = bits ^ jnp.right_shift(bits, shift)
    return (1 - 2 * (bits & 1)).astype(jnp.float32)


def scaled_cosine(turns):
    rest = turns - jnp.round(turns)
    square = rest * rest
    total = jnp.full_like(square, COS[-1])
    for c in COS[-2::-1]:
        total = total * square + c
    return total


def transform(blocks):
    stride = 1
    while stride < len(blocks):
        result = list(blocks)
        for i in range(len(blocks)):
            if not i & stride:
                result[i] = blocks[i] + blocks[i + stride]
                result[i + stride] = blocks[i] - blocks[i + stride]
        blocks = result
        stride *= 2
    return blocks


def inverse_factor(gram):
    size = gram.shape[0]
    row = lax.broadcasted_iota(jnp.int32, (8, size), 0)
    lane = lax.broadcasted_iota(jnp.int32, (8, size), 1)
    width = 2 * size
    sub = lax.broadcasted_iota(jnp.int32, (8, width), 0)
    groups = [
        jnp.concatenate(
            [(lane == row + 8 * g).astype(jnp.float32), gram[8 * g : 8 * g + 8]], axis=1
        )
        for g in range(size // 8)
    ]
    pivots = [jnp.ones((8, width), jnp.float32) for _ in groups]
    step = 8

    def spread(x):
        return jnp.broadcast_to(x, (8, width))

    for own in range(size // 8):
        first = size + own * step
        live = range(own, size // 8)
        rows = [spread(groups[own][k : k + 1]) for k in range(step)]
        cols = [
            {g: spread(groups[g][:, first + k : first + k + 1]) for g in live}
            for k in range(step)
        ]
        cross = {
            (k, m): spread(cols[m][own][k : k + 1]) for k in range(step) for m in range(k + 1)
        }
        for k in range(step):
            inverse = 1.0 / cross[k, k]
            pivots[own] = jnp.where(sub == k, cross[k, k], pivots[own])
            factor = {later: cross[later, k] * inverse for later in range(k + 1, step)}
            for later in range(k + 1, step):
                for m in range(k + 1, later + 1):
                    cross[later, m] = cross[later, m] - factor[later] * cross[m, k]
            for later in range(k + 1, step):
                rows[later] = rows[later] - factor[later] * rows[k]
                for g in live:
                    cols[later][g] = cols[later][g] - factor[later] * cols[k][g]
            for g in live:
                weight = cols[k][g] * inverse
                if g == own:
                    weight = jnp.where(sub > k, weight, 0.0)
                groups[g] = groups[g] - weight * rows[k]
    scaled = [g / jnp.sqrt(p) for g, p in zip(groups, pivots)]
    return jnp.concatenate(scaled, axis=0)[:, :size]


def kernel(
    feats, samps, emb_in, bits_in, perm_in, gauss_in, scale_in, phase_in, basis_in,
    proj_out, grown_out, gram_out,
    emb, bits, perm, gauss, scale, phase, basis,
    table, small, features, score_send, score_recv, proj, upd_send, upd_recv,
    grown, quarters, grams,
    s1, r1, s2, r2, s3, r3, s4, r4, s5, r5, s6, r6, loads, emb_loads, stores,
):
    me = lax.axis_index("feat")
    my = lax.axis_index("samp")
    rows, width = emb.shape
    order = basis.shape[0]
    chunk = rows // feats
    span = width // samps

    def chunk_rows(slot):
        return pl.ds(pl.multiple_of(slot * chunk, chunk), chunk)

    def emb_load(slot):
        where = chunk_rows(slot)
        return pltpu.make_async_copy(emb_in.at[where, :], emb.at[where, :], emb_loads.at[slot])

    pairs = (
        (perm_in, perm), (bits_in, bits), (gauss_in, gauss), (scale_in, scale),
        (phase_in, phase), (basis_in, basis),
    )
    parameters = [
        pltpu.make_async_copy(source, place, loads.at[n])
        for n, (source, place) in enumerate(pairs)
    ]
    for load in parameters:
        load.start()
    for d in range(1, feats + 1):
        emb_load(lax.rem(me + d, feats)).start()
    barrier = pltpu.get_barrier_semaphore()
    for d in range(1, feats):
        pl.semaphore_signal(
            barrier, inc=1, device_id={"feat": lax.rem(me + d, feats)}, device_id_type=MESH
        )
    for d in range(1, samps):
        pl.semaphore_signal(
            barrier, inc=1, device_id={"samp": lax.rem(my + d, samps)}, device_id_type=MESH
        )

    for load in parameters:
        load.wait()
    places = perm[...]
    base = parity_sign(lax.broadcasted_iota(jnp.int32, (128, width), 0) & places & 127).astype(
        jnp.bfloat16
    )
    for a in range(width // 128):
        flips = parity_sign(jnp.right_shift(places, 7) & a).astype(jnp.bfloat16)
        table[a * 128 : (a + 1) * 128, :] = base * flips
    square = (BLOCK, BLOCK)
    small[...] = parity_sign(
        lax.broadcasted_iota(jnp.int32, square, 0) & lax.broadcasted_iota(jnp.int32, square, 1)
    ).astype(jnp.bfloat16)
    signs = (2 * bits[...] - 1).astype(jnp.float32).astype(jnp.bfloat16)
    gains = gauss[...]
    rate = scale[...] * (1.0 / (2.0 * math.pi * width))
    offset = phase[...] * (1.0 / (2.0 * math.pi))
    basis_low = basis[...].astype(jnp.bfloat16)

    def copy(src, dst, send, recv, axis, to):
        return pltpu.make_async_remote_copy(
            src_ref=src, dst_ref=dst, send_sem=send, recv_sem=recv,
            device_id={axis: to}, device_id_type=MESH,
        )

    def score_copy(to):
        return copy(score_send.at[to], score_recv.at[me], s1.at[to], r1.at[me], "feat", to)

    def chunk_scores(i):
        at = lax.rem(me + 1 + i, feats)
        where = chunk_rows(at)
        emb_load(at).wait()
        signed = emb[where, :] * signs
        first = jnp.dot(signed, table[...], preferred_element_type=jnp.float32)
        first = first.astype(jnp.bfloat16).astype(jnp.float32)
        mixed = (first * gains).astype(jnp.bfloat16)
        stacked = jnp.concatenate(
            [mixed[:, n * BLOCK : (n + 1) * BLOCK] for n in range(width // BLOCK)], axis=0
        )
        stacked = jnp.dot(stacked, small[...], preferred_element_type=jnp.float32)
        parts = [stacked[n * chunk : (n + 1) * chunk] for n in range(width // BLOCK)]
        for n, part in enumerate(transform(parts)):
            cols = slice(n * BLOCK, (n + 1) * BLOCK)
            turns = part * rate[:, cols] + offset[:, cols]
            features[where, cols] = scaled_cosine(turns).astype(jnp.bfloat16)
        score_send[at] = lax.dot_general(
            basis_low, features[where, :], (((1,), (1,)), ((), ())),
            preferred_element_type=jnp.float32,
        )
        return at

    def chunk_step(i, carry):
        at = chunk_scores(i)

        @pl.when(i < feats - 1)
        def _():
            score_copy(at).start()

        return carry

    to = chunk_scores(0)
    pl.semaphore_wait(barrier, feats + samps - 2)
    score_copy(to).start()
    lax.fori_loop(1, feats, chunk_step, 0)

    total = score_send[me]
    for d in range(1, feats):
        source = lax.rem(me + d, feats)
        copy(
            score_send.at[source], score_recv.at[source], s1.at[source], r1.at[source],
            "feat", source,
        ).wait_recv()
        total = total + score_recv[source]
    proj[me] = total * (1.0 / math.sqrt(width * feats))

    def proj_copy(slot, to):
        return copy(proj.at[slot], proj.at[slot], s2.at[to], r2.at[slot], "feat", to)

    for d in range(1, feats):
        proj_copy(me, lax.rem(me + d, feats)).start()

    def add_rows(slot, first):
        where = chunk_rows(slot)
        low = proj[slot].astype(jnp.bfloat16)
        for q in range(samps):
            term = jnp.dot(
                low, features[where, q * span : (q + 1) * span],
                preferred_element_type=jnp.float32,
            )
            upd_send[q] = term if first else upd_send[q] + term

    add_rows(me, True)
    for d in range(1, feats):
        source = lax.rem(me + d, feats)
        proj_copy(source, source).wait_recv()
        add_rows(source, False)

    def upd_copy(to):
        return copy(upd_send.at[to], upd_recv.at[my], s3.at[to], r3.at[my], "samp", to)

    for d in range(1, samps):
        upd_copy(lax.rem(my + d, samps)).start()
    proj_store = pltpu.make_async_copy(proj, proj_out, stores.at[0])
    proj_store.start()
    total = upd_send[my]
    for d in range(1, samps):
        source = lax.rem(my + d, samps)
        copy(
            upd_send.at[source], upd_recv.at[source], s3.at[source], r3.at[source],
            "samp", source,
        ).wait_recv()
        total = total + upd_recv[source]
    own_cols = pl.ds(pl.multiple_of(my * span, span), span)
    grown[my] = basis[:, own_cols] + total * (1.0 / math.sqrt(rows * samps))

    block = grown[my]
    gram = lax.dot_general(
        block, block, (((1,), (1,)), ((), ())), precision=HIGHEST,
        preferred_element_type=jnp.float32,
    )
    half = order // 2
    quarters[my] = jnp.concatenate([gram[:half], gram[half:]], axis=1)

    def quarter_copy(slot, to):
        return copy(quarters.at[slot], quarters.at[slot], s6.at[to], r6.at[slot], "samp", to)

    def grown_copy(slot, to):
        return copy(grown.at[slot], grown.at[slot], s4.at[to], r4.at[slot], "samp", to)

    for d in range(1, samps):
        quarter_copy(my, lax.rem(my + d, samps)).start()
    for d in range(1, samps):
        grown_copy(my, lax.rem(my + d, samps)).start()
    for d in range(1, samps):
        source = lax.rem(my + d, samps)
        quarter_copy(source, source).wait_recv()
    packed = quarters[0]
    for slot in range(1, samps):
        packed = packed + quarters[slot]
    grams[me] = packed

    def gram_copy(slot, to):
        return copy(grams.at[slot], grams.at[slot], s5.at[to], r5.at[slot], "feat", to)

    for d in range(1, feats):
        gram_copy(me, lax.rem(me + d, feats)).start()
    for d in range(1, samps):
        source = lax.rem(my + d, samps)
        grown_copy(source, source).wait_recv()
    grown_store = pltpu.make_async_copy(grown, grown_out, stores.at[1])
    grown_store.start()
    for d in range(1, feats):
        source = lax.rem(me + d, feats)
        gram_copy(source, source).wait_recv()
    packed = grams[0]
    for slot in range(1, feats):
        packed = packed + grams[slot]
    gram_out[...] = packed * (1.0 / (width * feats))
    for d in range(1, feats):
        to = lax.rem(me + d, feats)
        score_copy(to).wait_send()
        proj_copy(me, to).wait_send()
        gram_copy(me, to).wait_send()
    proj_store.wait()
    grown_store.wait()
    for d in range(1, samps):
        to = lax.rem(my + d, samps)
        upd_copy(to).wait_send()
        quarter_copy(my, to).wait_send()
        grown_copy(my, to).wait_send()


def finish(
    proj_in, grown_in, packed, out, scores_out, proj, grown, result, loads, out_sems, score_sems
):
    feats, order, chunk = proj.shape
    samps, _, span = grown.shape
    proj_load = pltpu.make_async_copy(proj_in, proj, loads.at[0])
    grown_load = pltpu.make_async_copy(grown_in, grown, loads.at[1])
    proj_load.start()
    grown_load.start()
    proj_load.wait()
    stores = [
        pltpu.make_async_copy(
            proj.at[slot], scores_out.at[:, slot * chunk : (slot + 1) * chunk],
            score_sems.at[slot],
        )
        for slot in range(feats)
    ]
    for store in stores:
        store.start()
    halves = packed[...]
    gram = jnp.concatenate([halves[:, :order], halves[:, order:]], axis=0)
    inverse = inverse_factor(gram)
    grown_load.wait()
    for q in range(samps):
        result[q] = jnp.dot(
            inverse, grown[q], precision=HIGHEST, preferred_element_type=jnp.float32
        )
        store = pltpu.make_async_copy(
            result.at[q], out.at[:, q * span : (q + 1) * span], out_sems.at[q]
        )
        store.start()
        stores.append(store)
    for store in stores:
        store.wait()


def fused(feats, samps, embeddings, sign_bits, perms, gauss, scale, phase, basis):
    rows, width = embeddings.shape
    order = basis.shape[0]
    chunk, span = rows // feats, width // samps
    line = (1, width)
    whole = pl.BlockSpec(memory_space=pltpu.VMEM)
    far = pl.BlockSpec(memory_space=pltpu.HBM)
    f32, bf16, dma = jnp.float32, jnp.bfloat16, pltpu.SemaphoreType.DMA
    proj, grown, packed = pl.pallas_call(
        functools.partial(kernel, feats, samps),
        out_shape=(
            jax.ShapeDtypeStruct((feats, order, chunk), f32),
            jax.ShapeDtypeStruct((samps, order, span), f32),
            jax.ShapeDtypeStruct((order // 2, 2 * order), f32),
        ),
        in_specs=[far] * 7,
        out_specs=(far, far, whole),
        scratch_shapes=[
            pltpu.VMEM((rows, width), bf16),
            pltpu.VMEM(line, jnp.int32),
            pltpu.VMEM(line, jnp.int32),
            pltpu.VMEM(line, f32),
            pltpu.VMEM(line, f32),
            pltpu.VMEM(line, f32),
            pltpu.VMEM((order, width), f32),
            pltpu.VMEM((width, width), bf16),
            pltpu.VMEM((BLOCK, BLOCK), bf16),
            pltpu.VMEM((rows, width), bf16),
            pltpu.VMEM((feats, order, chunk), f32),
            pltpu.VMEM((feats, order, chunk), f32),
            pltpu.VMEM((feats, order, chunk), f32),
            pltpu.VMEM((samps, order, span), f32),
            pltpu.VMEM((samps, order, span), f32),
            pltpu.VMEM((samps, order, span), f32),
            pltpu.VMEM((samps, order // 2, 2 * order), f32),
            pltpu.VMEM((feats, order // 2, 2 * order), f32),
        ]
        + [dma((feats,))] * 4
        + [dma((samps,))] * 4
        + [dma((feats,))] * 2
        + [dma((samps,))] * 2
        + [dma((6,)), dma((feats,)), dma((2,))],
        compiler_params=pltpu.CompilerParams(
            collective_id=0, has_side_effects=True, vmem_limit_bytes=64 << 20
        ),
        name="oja",
    )(
        embeddings, sign_bits.reshape(line), perms.reshape(line), gauss.reshape(line),
        scale.reshape(line), phase.reshape(line), basis,
    )
    return pl.pallas_call(
        finish,
        out_shape=(
            jax.ShapeDtypeStruct((order, width), f32),
            jax.ShapeDtypeStruct((order, rows), f32),
        ),
        in_specs=[far, far, whole],
        out_specs=(far, far),
        scratch_shapes=[
            pltpu.VMEM((feats, order, chunk), f32),
            pltpu.VMEM((samps, order, span), f32),
            pltpu.VMEM((samps, order, span), f32),
            dma((2,)), dma((samps,)), dma((feats,)),
        ],
        name="finish",
    )(proj, grown, packed)


def sylvester(width):
    indices = lax.iota(jnp.int32, width)
    return parity_sign(indices[:, None] & indices[None, :]).astype(jnp.bfloat16)


def general(embeddings, sign_bits, perms, gauss, scale, phase, basis):
    rows, width = embeddings.shape
    table = sylvester(width)
    features_total = width * lax.axis_size("feat")
    span_total = rows * lax.axis_size("samp")
    signs = (2 * sign_bits - 1).astype(jnp.bfloat16)
    columns = parity_sign(lax.iota(jnp.int32, width)[:, None] & perms[0][None, :]).astype(
        jnp.bfloat16
    )
    first = jnp.dot(embeddings * signs, columns, preferred_element_type=jnp.float32)
    mixed = (first.astype(jnp.bfloat16) * gauss).astype(jnp.bfloat16)
    freq = jnp.dot(mixed, table, preferred_element_type=jnp.float32) * scale / width + phase
    features = (math.sqrt(2.0) * jnp.cos(freq)).astype(jnp.bfloat16)
    partial_scores = lax.dot_general(
        basis.astype(jnp.bfloat16), features, (((1,), (1,)), ((), ())),
        preferred_element_type=jnp.float32,
    )
    projections = lax.psum(partial_scores, "feat") / math.sqrt(features_total)
    update_part = jnp.dot(
        projections.astype(jnp.bfloat16), features, preferred_element_type=jnp.float32
    )
    grown = basis + lax.psum(update_part, "samp") / math.sqrt(span_total)
    gram = lax.psum(jnp.dot(grown, grown.T, precision=HIGHEST), "feat")
    lower = jnp.linalg.cholesky(gram / features_total)
    return jax.scipy.linalg.solve_triangular(lower, grown, lower=True), projections


def solution(mesh):
    feats, samps = mesh.shape["feat"], mesh.shape["samp"]

    def local(embeddings, sign_bits, perms, gauss, scale, phase, basis):
        rows, width = embeddings.shape
        fits = (
            rows % (feats * 128) == 0
            and width % (samps * 128) == 0
            and width % BLOCK == 0
            and perms.shape[0] == 1
            and basis.shape[0] == 64
            and 1 < feats
            and 1 < samps
        )
        body = functools.partial(fused, feats, samps) if fits else general
        return body(embeddings, sign_bits, perms, gauss, scale, phase, basis)

    placed = (
        P(("grp", "samp"), None),
        P("feat"),
        P("feat", None),
        P("feat"),
        P("feat"),
        P("feat"),
        P("grp", "feat"),
    )
    return jax.shard_map(
        local,
        mesh=mesh,
        in_specs=placed,
        out_specs=(P("grp", "feat"), P("grp", "samp")),
        check_vma=False,
    )
```

```python
import functools
import math

import jax
import jax.numpy as jnp
import numpy as np
from jax import lax
from jax.experimental import pallas as pl
from jax.experimental.pallas import tpu as pltpu
from jax.sharding import PartitionSpec as P

MESH = pl.DeviceIdType.MESH
BLOCK = 256
HIGHEST = lax.Precision.HIGHEST


def cosine_coefficients(degree):
    nodes = np.cos(np.pi * (np.arange(400) + 0.5) / 400)
    squares = (nodes + 1) / 8
    fitted = np.polynomial.Chebyshev.fit(
        squares, np.cos(2 * np.pi * np.sqrt(squares)), degree, domain=[0, 0.25]
    )
    return [float(c) * math.sqrt(2.0) for c in fitted.convert(kind=np.polynomial.Polynomial).coef]


COS = cosine_coefficients(6)


def parity_sign(bits):
    for shift in (8, 4, 2, 1):
        bits = bits ^ jnp.right_shift(bits, shift)
    return (1 - 2 * (bits & 1)).astype(jnp.float32)


def scaled_cosine(turns):
    rest = turns - jnp.round(turns)
    square = rest * rest
    total = jnp.full_like(square, COS[-1])
    for c in COS[-2::-1]:
        total = total * square + c
    return total


def transform(blocks):
    stride = 1
    while stride < len(blocks):
        result = list(blocks)
        for i in range(len(blocks)):
            if not i & stride:
                result[i] = blocks[i] + blocks[i + stride]
                result[i + stride] = blocks[i] - blocks[i + stride]
        blocks = result
        stride *= 2
    return blocks


def split(x):
    high = x.astype(jnp.bfloat16)
    rest = x - high.astype(jnp.float32)
    middle = rest.astype(jnp.bfloat16)
    low = (rest - middle.astype(jnp.float32)).astype(jnp.bfloat16)
    return high, middle, low


def inverse_factor(gram):
    size = gram.shape[0]
    row = lax.broadcasted_iota(jnp.int32, (8, size), 0)
    lane = lax.broadcasted_iota(jnp.int32, (8, size), 1)
    width = 2 * size
    sub = lax.broadcasted_iota(jnp.int32, (8, width), 0)
    groups = [
        jnp.concatenate(
            [(lane == row + 8 * g).astype(jnp.float32), gram[8 * g : 8 * g + 8]], axis=1
        )
        for g in range(size // 8)
    ]
    pivots = [jnp.ones((8, width), jnp.float32) for _ in groups]
    step = 8

    def spread(x):
        return jnp.broadcast_to(x, (8, width))

    for own in range(size // 8):
        first = size + own * step
        live = range(own, size // 8)
        rows = [spread(groups[own][k : k + 1]) for k in range(step)]
        cols = [
            {g: spread(groups[g][:, first + k : first + k + 1]) for g in live}
            for k in range(step)
        ]
        cross = {
            (k, m): spread(cols[m][own][k : k + 1]) for k in range(step) for m in range(k + 1)
        }
        for k in range(step):
            inverse = 1.0 / cross[k, k]
            pivots[own] = jnp.where(sub == k, cross[k, k], pivots[own])
            factor = {later: cross[later, k] * inverse for later in range(k + 1, step)}
            for later in range(k + 1, step):
                for m in range(k + 1, later + 1):
                    cross[later, m] = cross[later, m] - factor[later] * cross[m, k]
            for later in range(k + 1, step):
                rows[later] = rows[later] - factor[later] * rows[k]
                for g in live:
                    cols[later][g] = cols[later][g] - factor[later] * cols[k][g]
            for g in live:
                weight = cols[k][g] * inverse
                if g == own:
                    weight = jnp.where(sub > k, weight, 0.0)
                groups[g] = groups[g] - weight * rows[k]
    scaled = [g / jnp.sqrt(p) for g, p in zip(groups, pivots)]
    return jnp.concatenate(scaled, axis=0)[:, :size]


def kernel(
    feats, samps, emb_in, bits_in, perm_in, gauss_in, scale_in, phase_in, basis_in,
    proj_out, grown_out, gram_out,
    emb, bits, perm, gauss, scale, phase, basis,
    table, small, features, score_send, score_recv, proj, upd_send, upd_recv,
    grown, quarters, grams,
    s1, r1, s2, r2, s3, r3, s4, r4, s5, r5, s6, r6, loads, emb_loads, stores,
):
    me = lax.axis_index("feat")
    my = lax.axis_index("samp")
    rows, width = emb.shape
    order = basis.shape[0]
    chunk = rows // feats
    span = width // samps

    def chunk_rows(slot):
        return pl.ds(pl.multiple_of(slot * chunk, chunk), chunk)

    def emb_load(slot):
        where = chunk_rows(slot)
        return pltpu.make_async_copy(emb_in.at[where, :], emb.at[where, :], emb_loads.at[slot])

    pairs = (
        (perm_in, perm), (bits_in, bits), (gauss_in, gauss), (scale_in, scale),
        (phase_in, phase), (basis_in, basis),
    )
    parameters = [
        pltpu.make_async_copy(source, place, loads.at[n])
        for n, (source, place) in enumerate(pairs)
    ]
    for load in parameters:
        load.start()
    for d in range(1, feats + 1):
        emb_load(lax.rem(me + d, feats)).start()
    barrier = pltpu.get_barrier_semaphore()
    for d in range(1, feats):
        pl.semaphore_signal(
            barrier, inc=1, device_id={"feat": lax.rem(me + d, feats)}, device_id_type=MESH
        )
    for d in range(1, samps):
        pl.semaphore_signal(
            barrier, inc=1, device_id={"samp": lax.rem(my + d, samps)}, device_id_type=MESH
        )

    for load in parameters:
        load.wait()
    places = perm[...]
    base = parity_sign(lax.broadcasted_iota(jnp.int32, (128, width), 0) & places & 127).astype(
        jnp.bfloat16
    )
    for a in range(width // 128):
        flips = parity_sign(jnp.right_shift(places, 7) & a).astype(jnp.bfloat16)
        table[a * 128 : (a + 1) * 128, :] = base * flips
    square = (BLOCK, BLOCK)
    small[...] = parity_sign(
        lax.broadcasted_iota(jnp.int32, square, 0) & lax.broadcasted_iota(jnp.int32, square, 1)
    ).astype(jnp.bfloat16)
    signs = (2 * bits[...] - 1).astype(jnp.float32).astype(jnp.bfloat16)
    gains = gauss[...]
    rate = scale[...] * (1.0 / (2.0 * math.pi * width))
    offset = phase[...] * (1.0 / (2.0 * math.pi))
    basis_low = basis[...].astype(jnp.bfloat16)

    def copy(src, dst, send, recv, axis, to):
        return pltpu.make_async_remote_copy(
            src_ref=src, dst_ref=dst, send_sem=send, recv_sem=recv,
            device_id={axis: to}, device_id_type=MESH,
        )

    def score_copy(to):
        return copy(score_send.at[to], score_recv.at[me], s1.at[to], r1.at[me], "feat", to)

    def chunk_scores(i):
        at = lax.rem(me + 1 + i, feats)
        where = chunk_rows(at)
        emb_load(at).wait()
        signed = emb[where, :] * signs
        first = jnp.dot(signed, table[...], preferred_element_type=jnp.float32)
        first = first.astype(jnp.bfloat16).astype(jnp.float32)
        mixed = (first * gains).astype(jnp.bfloat16)
        stacked = jnp.concatenate(
            [mixed[:, n * BLOCK : (n + 1) * BLOCK] for n in range(width // BLOCK)], axis=0
        )
        stacked = jnp.dot(stacked, small[...], preferred_element_type=jnp.float32)
        parts = [stacked[n * chunk : (n + 1) * chunk] for n in range(width // BLOCK)]
        for n, part in enumerate(transform(parts)):
            cols = slice(n * BLOCK, (n + 1) * BLOCK)
            turns = part * rate[:, cols] + offset[:, cols]
            features[where, cols] = scaled_cosine(turns).astype(jnp.bfloat16)
        score_send[at] = lax.dot_general(
            basis_low, features[where, :], (((1,), (1,)), ((), ())),
            preferred_element_type=jnp.float32,
        )
        return at

    def chunk_step(i, carry):
        at = chunk_scores(i)

        @pl.when(i < feats - 1)
        def _():
            score_copy(at).start()

        return carry

    to = chunk_scores(0)
    pl.semaphore_wait(barrier, feats + samps - 2)
    score_copy(to).start()
    lax.fori_loop(1, feats, chunk_step, 0)

    total = score_send[me]
    for d in range(1, feats):
        source = lax.rem(me + d, feats)
        copy(
            score_send.at[source], score_recv.at[source], s1.at[source], r1.at[source],
            "feat", source,
        ).wait_recv()
        total = total + score_recv[source]
    proj[me] = total * (1.0 / math.sqrt(width * feats))

    def proj_copy(slot, to):
        return copy(proj.at[slot], proj.at[slot], s2.at[to], r2.at[slot], "feat", to)

    for d in range(1, feats):
        proj_copy(me, lax.rem(me + feats - d, feats)).start()

    def upd_copy(to):
        return copy(upd_send.at[to], upd_recv.at[my], s3.at[to], r3.at[my], "samp", to)

    def add_rows(slot, first, last):
        where = chunk_rows(slot)
        low = proj[slot].astype(jnp.bfloat16)
        for q in range(samps):
            term = jnp.dot(
                low, features[where, q * span : (q + 1) * span],
                preferred_element_type=jnp.float32,
            )
            upd_send[q] = term if first else upd_send[q] + term
            if last:

                @pl.when(my != q)
                def _():
                    upd_copy(q).start()

    add_rows(me, True, False)
    for d in range(1, feats):
        source = lax.rem(me + d, feats)
        proj_copy(source, source).wait_recv()
        add_rows(source, False, d == feats - 1)

    proj_store = pltpu.make_async_copy(proj, proj_out, stores.at[0])
    proj_store.start()
    total = upd_send[my]
    for d in range(1, samps):
        source = lax.rem(my + d, samps)
        copy(
            upd_send.at[source], upd_recv.at[source], s3.at[source], r3.at[source],
            "samp", source,
        ).wait_recv()
        total = total + upd_recv[source]
    own_cols = pl.ds(pl.multiple_of(my * span, span), span)
    grown[my] = basis[:, own_cols] + total * (1.0 / math.sqrt(rows * samps))

    block = grown[my]
    gram = lax.dot_general(
        block, block, (((1,), (1,)), ((), ())), precision=HIGHEST,
        preferred_element_type=jnp.float32,
    )
    half = order // 2
    quarters[my] = jnp.concatenate([gram[:half], gram[half:]], axis=1)

    def quarter_copy(slot, to):
        return copy(quarters.at[slot], quarters.at[slot], s6.at[to], r6.at[slot], "samp", to)

    def grown_copy(slot, to):
        return copy(grown.at[slot], grown.at[slot], s4.at[to], r4.at[slot], "samp", to)

    for d in range(1, samps):
        quarter_copy(my, lax.rem(my + d, samps)).start()
    for d in range(1, samps):
        source = lax.rem(my + d, samps)
        quarter_copy(source, source).wait_recv()
    packed = quarters[0]
    for slot in range(1, samps):
        packed = packed + quarters[slot]
    grams[me] = packed

    def gram_copy(slot, to):
        return copy(grams.at[slot], grams.at[slot], s5.at[to], r5.at[slot], "feat", to)

    for d in range(1, feats):
        gram_copy(me, lax.rem(me + d, feats)).start()
    for d in range(1, samps):
        grown_copy(my, lax.rem(my + d, samps)).start()
    for d in range(1, samps):
        source = lax.rem(my + d, samps)
        grown_copy(source, source).wait_recv()
    grown_store = pltpu.make_async_copy(grown, grown_out, stores.at[1])
    grown_store.start()
    for d in range(1, feats):
        source = lax.rem(me + d, feats)
        gram_copy(source, source).wait_recv()
    packed = grams[0]
    for slot in range(1, feats):
        packed = packed + grams[slot]
    gram_out[...] = packed * (1.0 / (width * feats))
    for d in range(1, feats):
        to = lax.rem(me + d, feats)
        score_copy(to).wait_send()
        proj_copy(me, to).wait_send()
        gram_copy(me, to).wait_send()
    proj_store.wait()
    grown_store.wait()
    for d in range(1, samps):
        to = lax.rem(my + d, samps)
        upd_copy(to).wait_send()
        quarter_copy(my, to).wait_send()
        grown_copy(my, to).wait_send()


def finish(
    proj_in, grown_in, packed, out, scores_out, proj, grown, result, loads, out_sems, score_sems
):
    feats, order, chunk = proj.shape
    samps, _, span = grown.shape
    proj_load = pltpu.make_async_copy(proj_in, proj, loads.at[0])
    grown_load = pltpu.make_async_copy(grown_in, grown, loads.at[1])
    proj_load.start()
    grown_load.start()
    proj_load.wait()
    stores = [
        pltpu.make_async_copy(
            proj.at[slot], scores_out.at[:, slot * chunk : (slot + 1) * chunk],
            score_sems.at[slot],
        )
        for slot in range(feats)
    ]
    for store in stores:
        store.start()
    halves = packed[...]
    gram = jnp.concatenate([halves[:, :order], halves[:, order:]], axis=0)
    inverse = inverse_factor(gram)
    high, middle, low = split(inverse)
    left = jnp.concatenate([high, high, middle, high, middle, low], axis=1)
    grown_load.wait()
    for q in range(samps):
        high, middle, low = split(grown[q])
        right = jnp.concatenate([high, middle, high, low, middle, high], axis=0)
        result[q] = jnp.dot(left, right, preferred_element_type=jnp.float32)
        store = pltpu.make_async_copy(
            result.at[q], out.at[:, q * span : (q + 1) * span], out_sems.at[q]
        )
        store.start()
        stores.append(store)
    for store in stores:
        store.wait()


def fused(feats, samps, embeddings, sign_bits, perms, gauss, scale, phase, basis):
    rows, width = embeddings.shape
    order = basis.shape[0]
    chunk, span = rows // feats, width // samps
    line = (1, width)
    whole = pl.BlockSpec(memory_space=pltpu.VMEM)
    far = pl.BlockSpec(memory_space=pltpu.HBM)
    f32, bf16, dma = jnp.float32, jnp.bfloat16, pltpu.SemaphoreType.DMA
    proj, grown, packed = pl.pallas_call(
        functools.partial(kernel, feats, samps),
        out_shape=(
            jax.ShapeDtypeStruct((feats, order, chunk), f32),
            jax.ShapeDtypeStruct((samps, order, span), f32),
            jax.ShapeDtypeStruct((order // 2, 2 * order), f32),
        ),
        in_specs=[far] * 7,
        out_specs=(far, far, whole),
        scratch_shapes=[
            pltpu.VMEM((rows, width), bf16),
            pltpu.VMEM(line, jnp.int32),
            pltpu.VMEM(line, jnp.int32),
            pltpu.VMEM(line, f32),
            pltpu.VMEM(line, f32),
            pltpu.VMEM(line, f32),
            pltpu.VMEM((order, width), f32),
            pltpu.VMEM((width, width), bf16),
            pltpu.VMEM((BLOCK, BLOCK), bf16),
            pltpu.VMEM((rows, width), bf16),
            pltpu.VMEM((feats, order, chunk), f32),
            pltpu.VMEM((feats, order, chunk), f32),
            pltpu.VMEM((feats, order, chunk), f32),
            pltpu.VMEM((samps, order, span), f32),
            pltpu.VMEM((samps, order, span), f32),
            pltpu.VMEM((samps, order, span), f32),
            pltpu.VMEM((samps, order // 2, 2 * order), f32),
            pltpu.VMEM((feats, order // 2, 2 * order), f32),
        ]
        + [dma((feats,))] * 4
        + [dma((samps,))] * 4
        + [dma((feats,))] * 2
        + [dma((samps,))] * 2
        + [dma((6,)), dma((feats,)), dma((2,))],
        compiler_params=pltpu.CompilerParams(
            collective_id=0, has_side_effects=True, vmem_limit_bytes=64 << 20
        ),
        name="oja",
    )(
        embeddings, sign_bits.reshape(line), perms.reshape(line), gauss.reshape(line),
        scale.reshape(line), phase.reshape(line), basis,
    )
    return pl.pallas_call(
        finish,
        out_shape=(
            jax.ShapeDtypeStruct((order, width), f32),
            jax.ShapeDtypeStruct((order, rows), f32),
        ),
        in_specs=[far, far, whole],
        out_specs=(far, far),
        scratch_shapes=[
            pltpu.VMEM((feats, order, chunk), f32),
            pltpu.VMEM((samps, order, span), f32),
            pltpu.VMEM((samps, order, span), f32),
            dma((2,)), dma((samps,)), dma((feats,)),
        ],
        name="finish",
    )(proj, grown, packed)


def sylvester(width):
    indices = lax.iota(jnp.int32, width)
    return parity_sign(indices[:, None] & indices[None, :]).astype(jnp.bfloat16)


def general(embeddings, sign_bits, perms, gauss, scale, phase, basis):
    rows, width = embeddings.shape
    table = sylvester(width)
    features_total = width * lax.axis_size("feat")
    span_total = rows * lax.axis_size("samp")
    signs = (2 * sign_bits - 1).astype(jnp.bfloat16)
    columns = parity_sign(lax.iota(jnp.int32, width)[:, None] & perms[0][None, :]).astype(
        jnp.bfloat16
    )
    first = jnp.dot(embeddings * signs, columns, preferred_element_type=jnp.float32)
    mixed = (first.astype(jnp.bfloat16) * gauss).astype(jnp.bfloat16)
    freq = jnp.dot(mixed, table, preferred_element_type=jnp.float32) * scale / width + phase
    features = (math.sqrt(2.0) * jnp.cos(freq)).astype(jnp.bfloat16)
    partial_scores = lax.dot_general(
        basis.astype(jnp.bfloat16), features, (((1,), (1,)), ((), ())),
        preferred_element_type=jnp.float32,
    )
    projections = lax.psum(partial_scores, "feat") / math.sqrt(features_total)
    update_part = jnp.dot(
        projections.astype(jnp.bfloat16), features, preferred_element_type=jnp.float32
    )
    grown = basis + lax.psum(update_part, "samp") / math.sqrt(span_total)
    gram = lax.psum(jnp.dot(grown, grown.T, precision=HIGHEST), "feat")
    lower = jnp.linalg.cholesky(gram / features_total)
    return jax.scipy.linalg.solve_triangular(lower, grown, lower=True), projections


def solution(mesh):
    feats, samps = mesh.shape["feat"], mesh.shape["samp"]

    def local(embeddings, sign_bits, perms, gauss, scale, phase, basis):
        rows, width = embeddings.shape
        fits = (
            rows % (feats * 128) == 0
            and width % (samps * 128) == 0
            and width % BLOCK == 0
            and perms.shape[0] == 1
            and basis.shape[0] == 64
            and 1 < feats
            and 1 < samps
        )
        body = functools.partial(fused, feats, samps) if fits else general
        return body(embeddings, sign_bits, perms, gauss, scale, phase, basis)

    placed = (
        P(("grp", "samp"), None),
        P("feat"),
        P("feat", None),
        P("feat"),
        P("feat"),
        P("feat"),
        P("grp", "feat"),
    )
    return jax.shard_map(
        local,
        mesh=mesh,
        in_specs=placed,
        out_specs=(P("grp", "feat"), P("grp", "samp")),
        check_vma=False,
    )
```
